32 devices in a mesh: fsdp: 32 (over z, y, x, core).
Axes of the slice: x: 2, y: 2, z: 4, core: 2. Of those that a mesh axis runs over, the one named last changes fastest.
Arguments:
- tokens: bfloat16 [16384, 1024], P('fsdp'), may hold values from -6 to 6
- out_grad: bfloat16 [16384, 1024], P('fsdp'), may hold values from -6 to 6
- segments: int32 [16384], replicated, may hold values from 0 to 63, never falling along the last dimension, each value on 1 to 512 neighbouring positions
- seq_lengths: int32 [4], replicated, may hold values from 1 to 8192, 16384 in all
- ln1_gain: bfloat16 [1024], P('fsdp'), may hold values from 0.5 to 1.5
- ln1_bias: bfloat16 [1024], P('fsdp'), may hold values from -3 to 3
- w_qkv: bfloat16 [1024, 3072], P('fsdp'), may hold values from -0.1875 to 0.1875
- b_qv: bfloat16 [2048], P('fsdp'), may hold values from -3 to 3
- w_out: bfloat16 [1024, 1024], P('fsdp'), may hold values from -0.75 to 0.75
- b_out: bfloat16 [1024], P('fsdp'), may hold values from -3 to 3
- ln2_gain: bfloat16 [1024], P('fsdp'), may hold values from 0.5 to 1.5
- ln2_bias: bfloat16 [1024], P('fsdp'), may hold values from -3 to 3
- w_fc: bfloat16 [1024, 4096], P('fsdp'), may hold values from -0.1875 to 0.1875
- b_fc: bfloat16 [4096], P('fsdp'), may hold values from -3 to 3
- w_proj: bfloat16 [4096, 1024], P('fsdp'), may hold values from -0.09375 to 0.09375
- b_proj: bfloat16 [1024], P('fsdp'), may hold values from -3 to 3
Outputs:
- block_out: bfloat16 [16384, 1024], P('fsdp')
- tokens_grad: float32 [16384, 1024], P('fsdp')
- ln1_gain_grad: float32 [1024], P('fsdp')
- ln1_bias_grad: float32 [1024], P('fsdp')
- w_qkv_grad: float32 [1024, 3072], P('fsdp')
- b_qv_grad: float32 [2048], P('fsdp')
- w_out_grad: float32 [1024, 1024], P('fsdp')
- b_out_grad: float32 [1024], P('fsdp')
- ln2_gain_grad: float32 [1024], P('fsdp')
- ln2_bias_grad: float32 [1024], P('fsdp')
- w_fc_grad: float32 [1024, 4096], P('fsdp')
- b_fc_grad: float32 [4096], P('fsdp')
- w_proj_grad: float32 [4096, 1024], P('fsdp')
- b_proj_grad: float32 [1024], P('fsdp')
The draws below stay inside these ranges and needn't reach their ends.
Inputs may be any that keep to these rules, and one draw needn't show every extreme that they name: `segments`: document numbers never fall along the token stream; every document number is used, by 1 to 512 consecutive tokens, and one document has exactly 512. `seq_lengths`: the sequences lie end to end from token 0 and their lengths sum to 16384; the longest has exactly half of 16384.
All inputs are finite; a program needn't handle non-finite values.
Results may differ from the reference program's by a relative error of at most 0.011.
Values may be sent and summed in bfloat16 or wider, within the bound.
No kernel may reach another device: no remote copies, remote signals or barrier semaphores. Data moves between devices by JAX's collectives and lax.ppermute only.
A program may use at most 192 MiB of HBM per device.

```python
import math
import jax
import jax.numpy as jnp
import numpy as np
from jax import lax

D = 1024
HEADS = 16
HEAD_DIM = 64
FF = 4096
SEQ = 512
TOKENS = 16384
NSEQ = 4
DOCS = 64


def strengthened(entries, rng, source, target, blocks, factor):
    def block_of(dim):
        return (jnp.arange(entries.shape[dim]) // (entries.shape[dim] // blocks)).reshape((-1,) + (1,) * (entries.ndim - 1 - dim))

    near = jax.random.permutation(rng, blocks)[block_of(target)]
    second = (block_of(target) + blocks // 2) % blocks
    return jnp.where((block_of(source) == near) | (block_of(source) == second), factor * entries, entries)


def levels(rng, dims, shards, least, top_value):
    gain, own = 1.0, jax.random.fold_in(rng, 6)
    for axis_at, blocks in shards:
        draws = jnp.exp(jax.random.uniform(jax.random.fold_in(own, axis_at), (blocks,), jnp.float32, least / len(shards), top_value / len(shards)))
        gain = gain * jnp.repeat(draws, dims[axis_at] // blocks).reshape([-1 if axis == axis_at else 1 for axis in range(len(dims))])
    return gain


def split_up(amount, total, most, lean):
    portions = [(1 << 20) // math.isqrt(grade ** lean) + 1 for grade in range(2, amount + 1)]
    surplus, given = total - most - (amount - 1), [1] * (amount - 1)
    while surplus > 0:
        free = [i for i in range(amount - 1) if given[i] < most]
        mass, remaining = sum([portions[i] for i in free]), surplus
        for i in free:
            addition = min(most - given[i], max(1, remaining * portions[i] // mass), surplus)
            given[i] = given[i] + addition
            surplus = surplus - addition
    return np.array([most] + given)


def ragged_sizes(own_key, amount, total, limit, slope):
    if amount == 2:
        one = jax.random.randint(own_key, (), max(1, total - limit), min(limit, total - 1) + 1)
        return jnp.stack([one, total - one])
    tallies = jnp.asarray(split_up(amount, total, limit, slope), jnp.int32)
    pairs = (amount - 1) // 2
    source_of, receiver = tallies[1:1 + 2 * pairs:2], tallies[2:2 + 2 * pairs:2]
    slack = jnp.minimum(source_of - 1, limit - receiver)
    shifted = jax.random.randint(jax.random.fold_in(own_key, 1), (pairs,), 0, 1 << 20) % (slack + 1)
    tallies = tallies.at[1:1 + 2 * pairs:2].set(source_of - shifted).at[2:2 + 2 * pairs:2].set(receiver + shifted)
    return tallies[jax.random.permutation(jax.random.fold_in(own_key, 2), amount)]


def scatter_about(rng, extent, spread, most, pieces=(), held_as=jnp.bfloat16):
    gain = levels(rng, extent, pieces, -0.22, 0.18) if pieces else 1.0
    values = jax.random.normal(rng, extent, jnp.float32) * spread * gain
    return jnp.minimum(jnp.maximum(values, -most), most).astype(held_as)


def heavy_noise(rng, dims, scale, reach, pieces, heavy, held_as=jnp.bfloat16):
    array = scale * jax.random.normal(rng, dims, jnp.float32)
    if pieces:
        array = array * levels(rng, dims, pieces, -0.22, 0.18)
    return jnp.clip(strengthened(array, jax.random.fold_in(rng, 3), *heavy), -reach, reach).astype(held_as)


def setup_inputs(seed: int = 0) -> dict:
    seeds = jax.random.split(jax.random.key(seed), 17)
    return {
        "tokens": heavy_noise(seeds[0], (TOKENS, D), 1.0, 6.0, ((0, 32),), (0, 1, 32, 2.75)),
        "out_grad": heavy_noise(seeds[1], (TOKENS, D), 1.0, 6.0, ((0, 32),), (0, 1, 32, 2.75)),
        "segments": jnp.searchsorted(jnp.cumsum(ragged_sizes(seeds[2], DOCS, TOKENS, SEQ, 1)), jnp.arange(TOKENS), side="right").astype(jnp.int32),
        "seq_lengths": ragged_sizes(seeds[3], NSEQ, TOKENS, TOKENS // 2, 1).astype(jnp.int32),
        "ln1_gain": jnp.clip(1.0 + 0.1 * jax.random.normal(seeds[4], (D,), jnp.float32), 0.5, 1.5).astype(jnp.bfloat16),
        "ln1_bias": scatter_about(seeds[5], (D,), 0.5, 3.0, ((0, 32),)),
        "w_qkv": scatter_about(seeds[6], (D, 3 * D), D ** -0.5, 0.1875, ((0, 32),)),
        "b_qv": scatter_about(seeds[7], (2 * D,), 0.5, 3.0, ((0, 32),)),
        "w_out": scatter_about(seeds[8], (D, D), (D // 16) ** -0.5, 0.75, ((0, 32),)),
        "b_out": scatter_about(seeds[9], (D,), 0.5, 3.0, ((0, 32),)),
        "ln2_gain": jnp.clip(1.0 + 0.1 * jax.random.normal(seeds[10], (D,), jnp.float32), 0.5, 1.5).astype(jnp.bfloat16),
        "ln2_bias": scatter_about(seeds[11], (D,), 0.5, 3.0, ((0, 32),)),
        "w_fc": scatter_about(seeds[12], (D, FF), D ** -0.5, 0.1875, ((0, 32),)),
        "b_fc": scatter_about(seeds[13], (FF,), 0.5, 3.0, ((0, 32),)),
        "w_proj": scatter_about(seeds[14], (FF, D), FF ** -0.5, 0.09375, ((0, 32),)),
        "b_proj": scatter_about(seeds[15], (D,), 0.5, 3.0, ((0, 32),)),
    }


@jax.custom_vjp
def low(v):
    return lax.optimization_barrier(v.astype(jnp.bfloat16)).astype(jnp.float32)

@jax.custom_vjp
def low_back(v):
    return v

def low_keep(v):
    return (low(v), None)

def low_pass(kept, grad):
    return (grad,)

def back_keep(v):
    return (v, None)

def back_low(kept, grad):
    return (low(grad),)
low.defvjp(low_keep, low_pass)
low_back.defvjp(back_keep, back_low)

def matmul_high(left, right):
    return jnp.dot(left, right, precision=lax.Precision.HIGHEST, preferred_element_type=jnp.float32)

def layer_norm(values, gain_row, shift_row):
    centre = lax.optimization_barrier(jnp.mean(values, axis=-1, keepdims=True))
    centered = values - centre
    variance = lax.optimization_barrier(jnp.mean(centered * centered, axis=-1, keepdims=True))
    return centered * lax.rsqrt(variance + 1e-05) * gain_row + shift_row

def gelu_tanh(values):
    return 0.5 * values * (1.0 + jnp.tanh(0.7978845608028654 * (values + 0.044715 * values * values * values)))

def attention(query, keys, values, segments, seq_ids):
    block_rows = min(512, TOKENS)
    block_count = TOKENS // block_rows
    scale_factor = HEAD_DIM ** (-0.5)
    zero_pad = jnp.zeros((block_rows, HEADS, HEAD_DIM), jnp.float32)
    keys_padded = jnp.concatenate([zero_pad, keys], axis=0)
    values_padded = jnp.concatenate([zero_pad, values], axis=0)
    minus_ones = jnp.full((block_rows,), -1, jnp.int32)
    seg_padded = jnp.concatenate([minus_ones, segments.astype(jnp.int32)], axis=0)
    seq_padded = jnp.concatenate([minus_ones, seq_ids.astype(jnp.int32)], axis=0)

    def one_block(block_index):
        start = (block_index * block_rows).astype(jnp.int32)
        q_block = lax.dynamic_slice_in_dim(query, start, block_rows, 0)
        k_window = lax.dynamic_slice_in_dim(keys_padded, start, 2 * block_rows, 0)
        v_window = lax.dynamic_slice_in_dim(values_padded, start, 2 * block_rows, 0)
        q_seg = lax.dynamic_slice_in_dim(segments.astype(jnp.int32), start, block_rows, 0)
        k_seg = lax.dynamic_slice_in_dim(seg_padded, start, 2 * block_rows, 0)
        q_seq = lax.dynamic_slice_in_dim(seq_ids.astype(jnp.int32), start, block_rows, 0)
        k_seq = lax.dynamic_slice_in_dim(seq_padded, start, 2 * block_rows, 0)
        q_pos = start + jnp.arange(block_rows, dtype=jnp.int32)
        k_pos = start - block_rows + jnp.arange(2 * block_rows, dtype=jnp.int32)
        allowed = (q_seg[:, None] == k_seg[None, :]) & (q_seq[:, None] == k_seq[None, :])
        allowed = allowed & (k_pos[None, :] <= q_pos[:, None]) & (k_pos[None, :] >= 0)
        raw_scores = jnp.einsum('qhd,khd->hqk', q_block, k_window, precision=lax.Precision.HIGHEST) * scale_factor
        scores = low_back(raw_scores)
        masked = jnp.where(allowed[None, :, :], scores, -1e+30)
        top_score = lax.optimization_barrier(jnp.max(masked, axis=-1, keepdims=True))
        expo = jnp.exp(masked - top_score)
        probs = low(expo / lax.optimization_barrier(jnp.sum(expo, axis=-1, keepdims=True)))
        mixed = jnp.einsum('hqk,khd->qhd', probs, v_window, precision=lax.Precision.HIGHEST)
        return mixed.reshape(block_rows, D)
    blocks = lax.map(jax.checkpoint(one_block), jnp.arange(block_count, dtype=jnp.int32))
    return blocks.reshape(TOKENS, D)

def forward(tokens, ln1_gain, ln1_bias, w_qkv, b_qv, w_out, b_out, ln2_gain, ln2_bias, w_fc, b_fc, w_proj, b_proj, segments, seq_ids):
    hidden_one = low(layer_norm(tokens, ln1_gain, ln1_bias))
    bias_full = jnp.concatenate([b_qv[:D], jnp.zeros((D,), jnp.float32), b_qv[D:]])
    qkv = low_back(low(matmul_high(hidden_one, w_qkv) + bias_full))
    query = qkv[:, :D].reshape(TOKENS, HEADS, HEAD_DIM)
    keys = qkv[:, D:2 * D].reshape(TOKENS, HEADS, HEAD_DIM)
    values = qkv[:, 2 * D:].reshape(TOKENS, HEADS, HEAD_DIM)
    attended = low_back(low(attention(query, keys, values, segments, seq_ids)))
    branch = low_back(matmul_high(attended, w_out) + b_out)
    resid = tokens + branch
    hidden_two = low(layer_norm(resid, ln2_gain, ln2_bias))
    pre = low_back(matmul_high(hidden_two, w_fc) + b_fc)
    act = low(gelu_tanh(pre))
    mlp_out = low_back(matmul_high(act, w_proj) + b_proj)
    return resid + mlp_out

def reference(tokens, out_grad, segments, seq_lengths, ln1_gain, ln1_bias, w_qkv, b_qv, w_out, b_out, ln2_gain, ln2_bias, w_fc, b_fc, w_proj, b_proj):
    seq_ends = jnp.cumsum(seq_lengths).astype(jnp.int32)
    positions = jnp.arange(TOKENS, dtype=jnp.int32)
    seq_ids = jnp.searchsorted(seq_ends, positions, side='right').astype(jnp.int32)
    params = tuple((item.astype(jnp.float32) for item in (tokens, ln1_gain, ln1_bias, w_qkv, b_qv, w_out, b_out, ln2_gain, ln2_bias, w_fc, b_fc, w_proj, b_proj)))

    def wrapped(*inputs):
        return forward(*inputs, segments, seq_ids)
    result, pullback = jax.vjp(wrapped, *params)
    grads = pullback(out_grad.astype(jnp.float32))
    return (result.astype(jnp.bfloat16), grads[0], grads[1], grads[2], grads[3], grads[4], grads[5], grads[6], grads[7], grads[8], grads[9], grads[10], grads[11], grads[12])
```

```python
import functools

import jax
import jax.numpy as jnp
from jax import lax
from jax.experimental import pallas as pl
from jax.experimental.pallas import tpu as pltpu
from jax.sharding import PartitionSpec as P

HEAD_DIM = 64
SEQ = 512
LANES = 128
BLOCK = 256

NORM_EPS = 1e-05
GELU_COEF = 0.7978845608028654
GELU_CUBIC = 0.044715
MASK_FILL = -1e30
SCALE = HEAD_DIM ** (-0.5)


def from_behind(value, axis, steps):
    count = lax.axis_size(axis)
    initial, last = (max(0, -steps), min(count, count - steps))
    return lax.ppermute(value, axis, [(source, source + steps) for source in range(initial, last)])


def times_plain(left, right):
    return jnp.dot(left, right, preferred_element_type=jnp.float32)


def times_left_t(left, right):
    return lax.dot_general(
        left, right, (((0,), (0,)), ((), ())), preferred_element_type=jnp.float32
    )


def times_right_t(left, right):
    return lax.dot_general(
        left, right, (((1,), (1,)), ((), ())), preferred_element_type=jnp.float32
    )


def norm_parts(values):
    centre = jnp.mean(values, axis=-1, keepdims=True)
    centered = values - centre
    inverse = lax.rsqrt(jnp.mean(centered * centered, axis=-1, keepdims=True) + NORM_EPS)
    return (centered * inverse, inverse)


def norm_back(grad_out, normed, inverse, gain_row):
    scaled = grad_out * gain_row
    return inverse * (
        scaled
        - jnp.mean(scaled, axis=-1, keepdims=True)
        - normed * jnp.mean(scaled * normed, axis=-1, keepdims=True)
    )


def one_head(pair, low_lanes, head):
    keep = low_lanes if head == 0 else jnp.logical_not(low_lanes)
    return jnp.where(keep, pair, jnp.zeros_like(pair))


def forward_kernel(bias_ref, q_ref, k_ref, v_ref, pk_ref, pv_ref, out_ref, lse_ref):
    rows = q_ref.shape[0]
    low_lanes = lax.broadcasted_iota(jnp.int32, (1, LANES), 1) < HEAD_DIM
    keys = jnp.concatenate([pk_ref[...], k_ref[...]], axis=0)
    values = jnp.concatenate([pv_ref[...], v_ref[...]], axis=0)
    span = SEQ + BLOCK
    for block in range(rows // BLOCK):
        at = block * BLOCK
        k_block, v_block = keys[at : at + span], values[at : at + span]
        q_pair = q_ref[at : at + BLOCK, :] * jnp.bfloat16(SCALE)
        mixed = []
        for head in range(2):
            scores = times_right_t(k_block, one_head(q_pair, low_lanes, head)) + bias_ref[block]
            top = jnp.max(scores, axis=0, keepdims=True)
            expo = jnp.exp(scores - top)
            total = jnp.sum(expo, axis=0, keepdims=True)
            probs = (expo * (1.0 / total)).astype(jnp.bfloat16)
            mixed.append(times_left_t(probs, v_block))
            lse_ref[0, head : head + 1, at : at + BLOCK] = top + jnp.log(total)
        out_ref[at : at + BLOCK, :] = jnp.where(low_lanes, mixed[0], mixed[1]).astype(jnp.bfloat16)


def backward_kernel(
    bias_ref, q_ref, k_ref, v_ref, pk_ref, pv_ref, g_ref, lse_ref, dq_ref, own_ref, prior_ref, acc
):
    rows = q_ref.shape[0]
    low_lanes = lax.broadcasted_iota(jnp.int32, (1, LANES), 1) < HEAD_DIM
    keys = jnp.concatenate([pk_ref[...], k_ref[...]], axis=0)
    values = jnp.concatenate([pv_ref[...], v_ref[...]], axis=0)
    span = SEQ + BLOCK
    acc[...] = jnp.zeros_like(acc)
    for block in range(rows // BLOCK):
        at = block * BLOCK
        k_block, v_block = keys[at : at + span], values[at : at + span]
        q_pair = q_ref[at : at + BLOCK, :] * jnp.bfloat16(SCALE)
        g_pair = g_ref[at : at + BLOCK, :]
        d_query = jnp.zeros((BLOCK, LANES), jnp.float32)
        d_key = jnp.zeros((span, LANES), jnp.float32)
        d_value = jnp.zeros((span, LANES), jnp.float32)
        for head in range(2):
            q_head = one_head(q_pair, low_lanes, head)
            g_head = one_head(g_pair, low_lanes, head)
            scores = times_right_t(k_block, q_head) + bias_ref[block]
            probs = jnp.exp(scores - lse_ref[0, head : head + 1, at : at + BLOCK])
            d_probs = times_right_t(v_block, g_head)
            delta = jnp.sum(probs * d_probs, axis=0, keepdims=True)
            d_scores = (probs * (d_probs - delta)).astype(jnp.bfloat16)
            d_query = d_query + times_left_t(d_scores, one_head(k_block, low_lanes, head))
            d_key = d_key + times_plain(d_scores, q_head)
            d_value = d_value + times_plain(probs.astype(jnp.bfloat16), g_head)
        dq_ref[at : at + BLOCK, :] = (d_query * SCALE).astype(jnp.bfloat16)
        acc[0, at : at + span, :] += d_key
        acc[1, at : at + span, :] += d_value
    prior_ref[...] = acc[:, :SEQ, :].astype(jnp.bfloat16)
    own_ref[...] = acc[:, SEQ:, :]


def attention_forward(bias, qkv, prior):
    rows, width = qkv.shape[0], qkv.shape[1] // 3
    steps = width // LANES
    column = lambda third: pl.BlockSpec((rows, LANES), lambda h: (0, h + third * steps))
    return pl.pallas_call(
        forward_kernel,
        grid=(steps,),
        in_specs=[
            pl.BlockSpec(bias.shape, lambda h: (0, 0, 0)),
            column(0),
            column(1),
            column(2),
            column(0),
            column(1),
        ],
        out_specs=[column(0), pl.BlockSpec((1, 2, rows), lambda h: (h, 0, 0))],
        out_shape=[
            jax.ShapeDtypeStruct((rows, width), jnp.bfloat16),
            jax.ShapeDtypeStruct((steps, 2, rows), jnp.float32),
        ],
        cost_estimate=pl.CostEstimate(
            flops=8 * rows * width * (SEQ + BLOCK), bytes_accessed=12 * rows * width, transcendentals=0
        ),
        name="attention_forward",
    )(bias, qkv, qkv, qkv, prior, prior)


def attention_backward(bias, qkv, prior, grad_att, lse):
    rows, width = grad_att.shape
    steps = width // LANES
    column = lambda third: pl.BlockSpec((rows, LANES), lambda h: (0, h + third * steps))
    both = pl.BlockSpec((2, rows, LANES), lambda h: (0, 0, h))
    return pl.pallas_call(
        backward_kernel,
        grid=(steps,),
        in_specs=[
            pl.BlockSpec(bias.shape, lambda h: (0, 0, 0)),
            column(0),
            column(1),
            column(2),
            column(0),
            column(1),
            column(0),
            pl.BlockSpec((1, 2, rows), lambda h: (h, 0, 0)),
        ],
        out_specs=[column(0), both, both],
        out_shape=[
            jax.ShapeDtypeStruct((rows, width), jnp.bfloat16),
            jax.ShapeDtypeStruct((2, rows, width), jnp.float32),
            jax.ShapeDtypeStruct((2, SEQ, width), jnp.bfloat16),
        ],
        scratch_shapes=[pltpu.VMEM((2, SEQ + rows, LANES), jnp.float32)],
        cost_estimate=pl.CostEstimate(
            flops=20 * rows * width * (SEQ + BLOCK), bytes_accessed=24 * rows * width, transcendentals=0
        ),
        name="attention_backward",
    )(bias, qkv, qkv, qkv, prior, prior, grad_att, lse)


def score_bias(segments, seq_lengths, first_row, tok_rows):
    seq_ends = jnp.cumsum(seq_lengths)
    position = first_row - SEQ + jnp.arange(SEQ + tok_rows, dtype=jnp.int32)
    padded = jnp.concatenate([jnp.full((SEQ,), -1, jnp.int32), segments])
    segment = lax.dynamic_slice_in_dim(padded, first_row, SEQ + tok_rows, 0)
    sequence = jnp.sum((position[:, None] >= seq_ends[None, :]).astype(jnp.int32), axis=1)
    blocks = []
    for at in range(0, tok_rows, BLOCK):
        key, query = slice(at, at + SEQ + BLOCK), slice(at + SEQ, at + SEQ + BLOCK)
        allowed = segment[key][:, None] == segment[query][None, :]
        allowed = allowed & (sequence[key][:, None] == sequence[query][None, :])
        allowed = allowed & (position[key][:, None] <= position[query][None, :])
        allowed = allowed & (position[key][:, None] >= 0)
        blocks.append(jnp.where(allowed, 0.0, MASK_FILL).astype(jnp.float32))
    return jnp.stack(blocks)


def gather(part):
    return lax.all_gather(part, "fsdp", axis=0, tiled=True)


def scatter(whole):
    return lax.psum_scatter(whole, "fsdp", scatter_dimension=0, tiled=True)


def on_device(
    tokens,
    out_grad,
    segments,
    seq_lengths,
    ln1_gain,
    ln1_bias,
    w_qkv,
    b_qv,
    w_out,
    b_out,
    ln2_gain,
    ln2_bias,
    w_fc,
    b_fc,
    w_proj,
    b_proj,
):
    count = lax.axis_size("fsdp")
    tok_rows, width = tokens.shape
    hidden = w_fc.shape[1]
    share = w_qkv.shape[0]
    folds = hidden // width

    def fold_columns(part):
        return part.reshape(share, count, folds, share).transpose(0, 2, 1, 3).reshape(share, hidden)

    def unfold_columns(part):
        return part.reshape(share, folds, count, share).transpose(0, 2, 1, 3).reshape(share, hidden)

    small = jnp.concatenate(
        [ln1_gain, ln1_bias, b_qv, b_out, ln2_gain, ln2_bias, b_fc, b_proj]
    ).reshape(8 + folds, share)
    small = jnp.pad(small, ((0, LANES - 8 - folds), (0, 0))).T
    first = gather(jnp.concatenate([w_qkv, small], axis=1))
    proj_columns = w_proj.reshape(folds, share, width).transpose(1, 0, 2).reshape(share, hidden)
    second = gather(jnp.concatenate([w_out, fold_columns(w_fc), proj_columns], axis=1))

    qkv_full = first[:, : 3 * width]
    vectors = first[:, 3 * width :].T[: 8 + folds].astype(jnp.float32)
    gain_one, shift_one, out_bias = vectors[0], vectors[1], vectors[4]
    gain_two, shift_two, proj_bias = vectors[5], vectors[6], vectors[7 + folds]
    qv_bias = vectors[2:4].reshape(2, count, share).transpose(1, 0, 2).reshape(2 * width)
    fc_bias = vectors[7 : 7 + folds].reshape(hidden)
    out_full = second[:, :width]
    fc_full = second[:, width : width + hidden]
    proj_full = second[:, width + hidden :]

    first_row = lax.axis_index("fsdp") * tok_rows
    bias = score_bias(segments, seq_lengths, first_row, tok_rows)
    tokens_f = tokens.astype(jnp.float32)
    normed_one, inverse_one = norm_parts(tokens_f)
    hidden_one = (normed_one * gain_one + shift_one).astype(jnp.bfloat16)
    bias_full = jnp.concatenate([qv_bias[:width], jnp.zeros((width,), jnp.float32), qv_bias[width:]])
    qkv = (times_plain(hidden_one, qkv_full) + bias_full).astype(jnp.bfloat16)
    prior = from_behind(qkv[:, width:], "fsdp", 1)
    attended, lse = attention_forward(bias, qkv, prior)

    resid = tokens_f + times_plain(attended, out_full) + out_bias
    normed_two, inverse_two = norm_parts(resid)
    hidden_two = (normed_two * gain_two + shift_two).astype(jnp.bfloat16)
    pre = times_plain(hidden_two, fc_full) + fc_bias
    tanh_part = jnp.tanh(GELU_COEF * (pre + GELU_CUBIC * pre * pre * pre))
    act = (0.5 * pre * (1.0 + tanh_part)).astype(jnp.bfloat16)
    proj_w_grad = jnp.concatenate(
        [
            times_left_t(act[:, j * width : (j + 1) * width], out_grad).astype(jnp.bfloat16)
            for j in range(folds)
        ],
        axis=1,
    )
    proj_share = scatter(proj_w_grad).astype(jnp.float32)
    result = resid + jnp.concatenate([proj_bias[None]], 0)
    for j in range(folds):
        cols = slice(j * width, (j + 1) * width)
        result = result + times_plain(act[:, cols], proj_full[:, cols])
    result = result.astype(jnp.bfloat16)

    grad_top = out_grad.astype(jnp.float32)
    proj_b_grad = jnp.sum(grad_top, axis=0)
    slope = 0.5 * (1.0 + tanh_part) + 0.5 * pre * (1.0 - tanh_part * tanh_part) * GELU_COEF * (
        1.0 + 3.0 * GELU_CUBIC * pre * pre
    )
    grad_act = jnp.concatenate(
        [times_right_t(out_grad, proj_full[:, j * width : (j + 1) * width]) for j in range(folds)],
        axis=1,
    )
    grad_pre = (grad_act * slope).astype(jnp.bfloat16)
    fc_w_grad = times_left_t(hidden_two, grad_pre).astype(jnp.bfloat16)
    fc_b_grad = jnp.sum(grad_pre.astype(jnp.float32), axis=0)
    grad_hidden_two = times_right_t(grad_pre, fc_full)
    gain_two_grad = jnp.sum(grad_hidden_two * normed_two, axis=0)
    shift_two_grad = jnp.sum(grad_hidden_two, axis=0)
    grad_resid = grad_top + norm_back(grad_hidden_two, normed_two, inverse_two, gain_two)
    grad_branch = grad_resid.astype(jnp.bfloat16)
    out_w_grad = times_left_t(attended, grad_branch).astype(jnp.bfloat16)
    out_b_grad = jnp.sum(grad_branch.astype(jnp.float32), axis=0)
    grad_att = times_right_t(grad_branch, out_full).astype(jnp.bfloat16)

    query_grad, own_grads, prior_grads = attention_backward(bias, qkv, prior, grad_att, lse)
    back = from_behind(prior_grads, "fsdp", -1).astype(jnp.float32)
    pair_grads = (own_grads + back).astype(jnp.bfloat16)
    grad_qkv = jnp.concatenate([query_grad, pair_grads[0], pair_grads[1]], axis=1)
    qkv_w_grad = times_left_t(hidden_one, grad_qkv).astype(jnp.bfloat16)
    column_sums = jnp.sum(grad_qkv.astype(jnp.float32), axis=0)
    qv_b_grad = jnp.concatenate([column_sums[:width], column_sums[2 * width :]])
    grad_hidden_one = times_right_t(grad_qkv, qkv_full)
    gain_one_grad = jnp.sum(grad_hidden_one * normed_one, axis=0)
    shift_one_grad = jnp.sum(grad_hidden_one, axis=0)
    tokens_grad = grad_resid + norm_back(grad_hidden_one, normed_one, inverse_one, gain_one)

    vector_grads = jnp.concatenate(
        [
            gain_one_grad[None],
            shift_one_grad[None],
            qv_b_grad.reshape(count, 2, share).transpose(1, 0, 2).reshape(2, width),
            out_b_grad[None],
            gain_two_grad[None],
            shift_two_grad[None],
            fc_b_grad.reshape(folds, width),
            proj_b_grad[None],
        ],
        axis=0,
    ).astype(jnp.bfloat16)
    vector_grads = jnp.pad(vector_grads, ((0, LANES - 8 - folds), (0, 0))).T
    shares = scatter(
        jnp.concatenate([qkv_w_grad, out_w_grad, fc_w_grad, vector_grads], axis=1)
    ).astype(jnp.float32)
    edges = (3 * width, 4 * width, 4 * width + hidden)
    vectors = shares[:, edges[2] :].T[: 8 + folds].reshape(-1)
    at = [share * k for k in (0, 1, 2, 4, 5, 6, 7, 7 + folds, 8 + folds)]
    pieces = [vectors[at[k] : at[k + 1]] for k in range(8)]
    return (
        result,
        tokens_grad,
        pieces[0],
        pieces[1],
        shares[:, : edges[0]],
        pieces[2],
        shares[:, edges[0] : edges[1]],
        pieces[3],
        pieces[4],
        pieces[5],
        unfold_columns(shares[:, edges[1] : edges[2]]),
        pieces[6],
        proj_share.reshape(share, folds, width).transpose(1, 0, 2).reshape(folds * share, width),
        pieces[7],
    )


def solution(mesh):
    rows, flat = P("fsdp", None), P("fsdp")
    return jax.shard_map(
        on_device,
        mesh=mesh,
        in_specs=(rows, rows, P(), P(), flat, flat, rows, flat, rows)
        + (flat, flat, flat, rows, flat, rows, flat),
        out_specs=(rows, rows, flat, flat, rows, flat, rows)
        + (flat, flat, flat, rows, flat, rows, flat),
        check_vma=False,
    )
```
